32 devices in a mesh: dp: 2 (over y), seq: 16 (over z, x, core).
Axes of the slice: x: 2, y: 2, z: 4, core: 2. Of those that a mesh axis runs over, the one named last changes fastest.
Arguments:
- tokens: bfloat16 [2, 8192, 1024], P('dp', 'seq'), may hold values from -50 to 50
- w_query: bfloat16 [1024, 1024], P(None, 'dp'), may hold values from -0.1875 to 0.1875
- w_key: bfloat16 [1024, 1024], P(None, 'dp'), may hold values from -0.1875 to 0.1875
- w_value: bfloat16 [1024, 1024], P(None, 'dp'), may hold values from -0.1875 to 0.1875
- w_out: bfloat16 [1024, 1024], P('dp'), may hold values from -0.1875 to 0.1875
- norm_gain: float32 [1024], replicated, may hold values from 0.1 to 1.9
Outputs:
- layer_out: bfloat16 [2, 8192, 1024], P('dp', 'seq')
The draws below stay inside these ranges and needn't reach their ends.
All inputs are finite; a program needn't handle non-finite values.
Results may differ from the reference program's by a relative error of at most 0.017.
Values may be sent and summed in bfloat16 or wider, within the bound.
A program may use at most 128 MiB of HBM per device.

```python
import math
import jax
import jax.numpy as jnp
from jax import lax

D = 1024
H = 8
DH = 128
TOK_DEV = 512
STACKS = 2
SEQ = 8192


def draw_tokens(key, part):
    first, second, third = jax.random.split(jax.random.fold_in(key, 11), 3)
    base = jnp.clip(jax.random.normal(first, (STACKS, SEQ, D), jnp.float32), -4.0, 4.0)
    row_scale = jnp.exp(jax.random.uniform(second, (STACKS, SEQ, 1), jnp.float32, 0.0, math.log(10.0)))
    col_scale = jnp.exp(jax.random.uniform(third, (D,), jnp.float32, 0.0, math.log(10.0)))
    return (base * row_scale * col_scale * 0.1).astype(jnp.bfloat16)


def steps_of(rng, extent, cuts, low, top_value):
    def one(dim, blocks):
        steps = jax.random.uniform(jax.random.fold_in(jax.random.fold_in(rng, 6), dim), (blocks,), jnp.float32, low / len(cuts), top_value / len(cuts))
        return jnp.repeat(jnp.exp(steps), extent[dim] // blocks).reshape((-1,) + (1,) * (len(extent) - dim - 1))

    level = one(*cuts[0])
    for cut in cuts[1:]:
        level = level * one(*cut)
    return level


def scatter_about(own_key, dims, spread, limit, cuts=(), kind=jnp.bfloat16):
    result = spread * jax.random.normal(own_key, dims, jnp.float32)
    if cuts:
        result = result * steps_of(own_key, dims, cuts, -0.22, 0.18)
    return jnp.clip(result, -limit, limit).astype(kind)


def setup_inputs(seed: int = 0) -> dict:
    key_of = jax.random.split(jax.random.key(seed), 7)
    tokens = draw_tokens(jax.random.fold_in(key_of[6], 71), 0)
    w_query = scatter_about(key_of[1], (D, D), D ** -0.5, 0.1875, ((1, 2),))
    w_key = scatter_about(key_of[2], (D, D), D ** -0.5, 0.1875, ((1, 2),))
    w_value = scatter_about(key_of[3], (D, D), D ** -0.5, 0.1875, ((1, 2),))
    w_out = scatter_about(key_of[4], (D, D), D ** -0.5, 0.1875, ((0, 2),))
    norm_gain = jnp.clip(1.0 + 0.18 * jax.random.normal(key_of[5], (D,), jnp.float32), 0.1, 1.9)
    return {"tokens": tokens, "w_query": w_query, "w_key": w_key, "w_value": w_value, "w_out": w_out, "norm_gain": norm_gain}


def rounded(value):
    return lax.optimization_barrier(value.astype(jnp.bfloat16)).astype(jnp.float32)

def inner_block(query_heads, key_heads, value_heads):
    length = query_heads.shape[1]
    block = min(length, 512)
    pieces = []
    for begin in range(0, length, block):
        finish = begin + block
        scores = jnp.einsum('hid,hjd->hij', query_heads[:, begin:finish].astype(jnp.float32), key_heads[:, :finish].astype(jnp.float32))
        row_ids = jnp.arange(begin, finish)[:, None]
        col_ids = jnp.arange(finish)[None, :]
        scores = rounded(jnp.where(col_ids <= row_ids, scores, 0.0))
        pieces.append(jnp.einsum('hij,hje->hie', scores, value_heads[:, :finish].astype(jnp.float32)))
    return jnp.concatenate(pieces, axis=1)

def reference(tokens, w_query, w_key, w_value, w_out, norm_gain):
    gain_heads = norm_gain.reshape(H, 1, DH)

    def one_stack(rows):

        def heads(weight):
            proj = jnp.dot(rows, weight, preferred_element_type=jnp.float32).astype(jnp.bfloat16)
            return proj.reshape(SEQ // TOK_DEV, TOK_DEV, H, DH).transpose(0, 2, 1, 3)
        blocks = (heads(w_query), heads(w_key), heads(w_value))

        def step(state, block):
            query_heads, key_heads, value_heads = block
            carried = jnp.einsum('htd,hde->hte', query_heads.astype(jnp.float32), rounded(state))
            mixed_raw = inner_block(query_heads, key_heads, value_heads) + carried
            scale = lax.rsqrt(lax.optimization_barrier(jnp.mean(mixed_raw * mixed_raw, axis=-1, keepdims=True)) + 1e-05)
            normed = (mixed_raw * scale * gain_heads).astype(jnp.bfloat16)
            state = state + jnp.einsum('htd,hte->hde', key_heads.astype(jnp.float32), value_heads.astype(jnp.float32))
            return (state, normed)
        start_state = jnp.zeros((H, DH, DH), jnp.float32)
        _, normed = lax.scan(step, start_state, blocks)
        normed = normed.transpose(0, 2, 1, 3).reshape(SEQ, D)
        return jnp.dot(normed, w_out, preferred_element_type=jnp.float32).astype(jnp.bfloat16)
    return lax.map(one_stack, tokens)
```

```python
import functools

import jax
import jax.numpy as jnp
from jax import lax
from jax.experimental import pallas as pl
from jax.experimental.pallas import tpu as pltpu
from jax.sharding import PartitionSpec as P

DH = 128
GROUP = 8
PLANE = 4
LAG = 3
DIRECT = ((1, 1, 1), (3, 1, 1))
MESH = pl.DeviceIdType.MESH
F32 = jnp.float32
BF16 = jnp.bfloat16


class Scan:
    def __init__(self, seq, outer, state, prior, out1, in1, total, in2, out3, sends, recvs):
        self.seq, self.outer = seq, outer
        self.state, self.prior = state, prior
        self.out1, self.in1, self.total, self.in2, self.out3 = out1, in1, total, in2, out3
        self.sends, self.recvs = sends, recvs
        self.share = state.shape[0] // PLANE
        self.me = lax.rem(seq, PLANE)
        self.row = seq // PLANE
        self.mine = self.rows(self.me)
        self.up, self.across, self.down = [], [], []

    def rows(self, owner):
        return pl.ds(pl.multiple_of(owner * self.share, 16), self.share)

    def copy(self, src, dst, index, target):
        return pltpu.make_async_remote_copy(
            src_ref=src,
            dst_ref=dst,
            send_sem=self.sends.at[index],
            recv_sem=self.recvs.at[index],
            device_id={"seq": target},
            device_id_type=MESH,
        )

    def plane(self, k):
        return lax.rem(self.me + k, PLANE)

    def begin(self):
        self.out1[...] = self.state[...].astype(BF16)
        for k in range(1, PLANE):
            target = self.plane(k)
            copy = self.copy(
                self.out1.at[self.rows(target), :], self.in1.at[k - 1], k - 1, self.seq - self.me + target
            )
            copy.start()
            self.up.append(copy)

    def middle(self):
        for copy in self.up:
            copy.wait_recv()
        total = self.state[self.mine, :]
        for k in range(1, PLANE):
            total = total + self.in1[k - 1].astype(F32)
        self.total[...] = total.astype(BF16)
        for k in range(1, self.outer):
            copy = self.copy(self.total, self.in2.at[k - 1], PLANE - 2 + k, self.seq + k * PLANE)
            pl.when(self.row + k < self.outer)(copy.start)
            self.across.append(copy)

    def last(self):
        before = jnp.zeros((self.share, DH), F32)
        for k in range(1, self.outer):
            pl.when(self.row >= k)(self.across[k - 1].wait_recv)
            before = before + jnp.where(self.row >= k, self.in2[k - 1].astype(F32), 0.0)
        parts = [(self.me, self.state[self.mine, :])]
        for k in range(1, PLANE):
            parts.append((self.plane(PLANE - k), self.in1[k - 1].astype(F32)))

        def prefix(target):
            result = before
            for source, part in parts:
                result = result + jnp.where(source < target, part, 0.0)
            return result.astype(BF16)

        for k in range(1, PLANE):
            target = self.plane(k)
            self.out3[k - 1] = prefix(target)
            copy = self.copy(
                self.out3.at[k - 1], self.prior.at[self.mine, :], PLANE - 3 + self.outer + k,
                self.seq - self.me + target,
            )
            copy.start()
            self.down.append(copy)
        self.prior[self.mine, :] = prefix(self.me)

    def end(self):
        for copy in self.down:
            copy.wait_recv()

    def close(self):
        for copy in self.up + self.down:
            copy.wait_send()
        for k in range(1, self.outer):
            pl.when(self.row + k < self.outer)(self.across[k - 1].wait_send)


def kernel(
    n, seqs, parts,
    tok_hbm, wq_hbm, wk_hbm, wv_hbm, wo_hbm, gain_ref, out_ref,
    tok, own, own_o, wide, wide_o, kvq, within, normed, acc,
    load_sem, sends, recvs, *scan_refs,
):
    dp, seq = lax.axis_index("dp"), lax.axis_index("seq")
    length, width = tok.shape
    cols = own.shape[2]
    pairs, lanes_per = wide.shape[2], wide.shape[4]
    outer = seqs // PLANE
    sources = [wk_hbm, wv_hbm, wq_hbm, wo_hbm]
    rank = lax.rem(seq, GROUP)
    core = lax.rem(seq, 2)
    xbit = lax.rem(seq // 2, 2)
    core_mate = seq + 1 - 2 * core
    x_mate = seq + 2 * (1 - 2 * xbit)
    zbit = lax.rem(seq // 4, 2)
    z_mate = seq + 4 * (1 - 2 * zbit)
    x_rank = rank + 2 * (1 - 2 * xbit)
    z_rank = rank + 4 * (1 - 2 * zbit)
    g_rank = z_rank + 2 * (1 - 2 * xbit)
    lanes = ("y", "x", "z", "g", "c0", "c1", "c2", "c3")

    loads = [pltpu.make_async_copy(tok_hbm, tok, load_sem.at[4])]
    for kind in range(4):
        dst = own.at[kind] if kind < 3 else own_o
        loads.append(pltpu.make_async_copy(sources[kind], dst, load_sem.at[kind]))
    for copy in loads:
        copy.start()

    barrier = pltpu.get_barrier_semaphore()
    for slot in range(1, n):
        pl.semaphore_signal(barrier, inc=1, device_id={"dp": lax.rem(dp + slot, n)}, device_id_type=MESH)
    for k in range(1, outer):
        pl.semaphore_signal(barrier, inc=1, device_id={"seq": lax.rem(seq + k * PLANE, seqs)}, device_id_type=MESH)
    place_in = lax.rem(seq, PLANE)
    for k in range(1, PLANE):
        mate = seq - place_in + lax.rem(place_in + k, PLANE)
        pl.semaphore_signal(barrier, inc=1, device_id={"seq": mate}, device_id_type=MESH)
    pl.semaphore_wait(barrier, n - 1 + outer - 1 + PLANE - 1)

    def direct(piece):
        return (piece[0], piece[2], piece[3]) in DIRECT

    def rows_of(piece, who):
        kind, _, p, s = piece
        region = (width if kind < 3 else lanes_per) // parts
        size = region // (2 if direct(piece) else GROUP)
        base = s * region + (p * lanes_per if kind == 3 else 0)
        return pl.ds(pl.multiple_of(base + who * size, 16), size)

    def place(piece, rows):
        kind, slot, p, _ = piece
        if kind < 3:
            return wide.at[slot - 1, kind, p, rows, :]
        return wide_o.at[slot - 1, rows, :]

    order, mark = [], {}
    for kinds in ((0, 1), (2,), (3,)):
        for p in range(pairs):
            for kind in kinds:
                order += [(kind, slot, p, s) for s in range(parts) for slot in range(1, n)]
                mark[kind, p] = len(order)
    remote, sent = {}, []

    def push(src, dst, index, target):
        copy = pltpu.make_async_remote_copy(
            src_ref=src, dst_ref=dst, send_sem=sends.at[index], recv_sem=recvs.at[index],
            device_id=target, device_id_type=MESH,
        )
        copy.start()
        sent.append(copy)
        return copy

    def index_of(name, piece):
        kind, slot, p, s = piece
        return (lanes.index(name), kind, slot - 1, p, s)

    for piece in order:
        kind, slot, p, _ = piece
        rows = rows_of(piece, core if direct(piece) else rank)
        if kind < 3:
            src = sources[kind].at[rows, pl.ds(p * lanes_per, lanes_per)]
        else:
            src = sources[kind].at[rows, :]
        remote["y", piece] = push(src, place(piece, rows), index_of("y", piece), {"dp": lax.rem(dp - slot + n, n)})

    def forward(name, piece, who, target):
        here = place(piece, rows_of(piece, who))
        remote[name, piece] = push(here, here, index_of(name, piece), {"seq": target})

    def relay(piece):
        remote["y", piece].wait_recv()
        if direct(piece):
            forward("c0", piece, core, core_mate)
            return
        forward("x", piece, rank, x_mate)
        forward("z", piece, rank, z_mate)
        forward("c0", piece, rank, core_mate)

    def relay_again(piece):
        if direct(piece):
            return
        even = (piece[1] + piece[3]) % 2 == 1
        remote["x", piece].wait_recv()
        if even:
            forward("g", piece, x_rank, z_mate)
        forward("c1", piece, x_rank, core_mate)
        remote["z", piece].wait_recv()
        if not even:
            forward("g", piece, z_rank, x_mate)
        forward("c2", piece, z_rank, core_mate)

    def relay_last(piece):
        if direct(piece):
            return
        remote["g", piece].wait_recv()
        forward("c3", piece, g_rank, core_mate)

    acts = (relay, relay_again, relay_last)
    done = [0, 0, 0]

    def go(*goals):
        goals = [max(at, goal * len(order) // 16) for at, goal in zip(done, goals)]
        goals[0] = max(goals)
        goals[1] = max(goals[1:])
        while any(at < goal for at, goal in zip(done, goals)):
            todo = [i for i in range(3) if done[i] < goals[i] and (i == 0 or done[i] < done[i - 1])]
            pick = min(todo, key=lambda i: done[i] + LAG * i)
            acts[pick](order[done[pick]])
            done[pick] += 1

    def ready(kind, p):
        assert done[2] >= mark[kind, p]
        for piece in order:
            if (piece[0], piece[2]) == (kind, p):
                for name in ("c0",) if direct(piece) else ("c0", "c1", "c2", "c3"):
                    remote[name, piece].wait_recv()

    def lane(i, size):
        return pl.ds(pl.multiple_of(i * size, 128), size)

    def project_own(kind):
        @pl.loop(0, pairs)
        def _(p):
            at = lane(p, lanes_per)
            kvq[kind, 0, :, at] = jnp.dot(tok[...], own[kind, :, at], preferred_element_type=F32).astype(BF16)

    def project(kind, p):
        for slot in range(1, n):
            at = pl.ds(p * lanes_per, lanes_per)
            kvq[kind, slot, :, at] = jnp.dot(
                tok[...], wide[slot - 1, kind, p], preferred_element_type=F32
            ).astype(BF16)

    per = lanes_per // DH

    def states(slot, first, count, ref, base):
        @pl.loop(0, count)
        def _(h):
            at = lane(first + h, DH)
            ref[pl.ds(pl.multiple_of(base + h * DH, DH), DH), :] = lax.dot_general(
                kvq[0, slot, :, at], kvq[1, slot, :, at], (((0,), (0,)), ((), ())), preferred_element_type=F32
            )

    half = length // 2

    def inner(slot, first, count):
        @pl.loop(0, count)
        def _(h):
            at = lane(first + h, DH)
            for begin in (0, half):
                end = begin + half
                scores = lax.dot_general(
                    kvq[2, slot, begin:end, at], kvq[0, slot, :end, at], (((1,), (1,)), ((), ())),
                    preferred_element_type=F32,
                )
                row = begin + lax.broadcasted_iota(jnp.int32, (half, end), 0)
                col = lax.broadcasted_iota(jnp.int32, (half, end), 1)
                scores = jnp.where(col <= row, scores, 0.0).astype(BF16)
                within[slot, begin:end, at] = jnp.dot(
                    scores, kvq[1, slot, :end, at], preferred_element_type=F32
                )

    heads = cols // DH

    def finish(slot, first, count, prior, base):
        owner = lax.rem(dp + slot, n)

        @pl.loop(0, count)
        def _(h):
            at = lane(first + h, DH)
            carried = jnp.dot(
                kvq[2, slot, :, at], prior[pl.ds(pl.multiple_of(base + h * DH, DH), DH), :],
                preferred_element_type=F32,
            )
            mixed = within[slot, :, at] + carried
            scale = lax.rsqrt(jnp.sum(mixed * mixed, axis=-1, keepdims=True) * (1.0 / DH) + 1e-05)
            gain = gain_ref[pl.ds(owner * heads + first + h, 1), :]
            normed[slot, :, at] = (mixed * scale * gain).astype(BF16)

    def join_own():
        @pl.loop(0, width // 256)
        def _(i):
            at = lane(i, 256)
            acc[:, at] = jnp.dot(normed[0], own_o[:, at], preferred_element_type=F32)

    def join(p):
        for slot in range(1, n):
            @pl.loop(0, width // 256)
            def _(i):
                at = lane(i, 256)
                span = pl.ds(p * lanes_per, lanes_per)
                part = acc[:, at] + jnp.dot(
                    normed[slot, :, span], wide_o[slot - 1, span, at], preferred_element_type=F32
                )
                if slot == n - 1 and p == pairs - 1:
                    out_ref[:, at] = part.astype(BF16)
                else:
                    acc[:, at] = part

    size = len(scan_refs) // (1 + pairs)
    scans = [Scan(seq, outer, *scan_refs[i * size:(i + 1) * size]) for i in range(1 + pairs)]
    scan_a, scan_b = scans[0], scans[1:]

    def states_b(p):
        for slot in range(1, n):
            states(slot, p * per, per, scan_b[p].state, (slot - 1) * lanes_per)
        scan_b[p].begin()

    def inner_b(p):
        for slot in range(1, n):
            inner(slot, p * per, per)

    def finish_b(p):
        scan_b[p].end()
        for slot in range(1, n):
            finish(slot, p * per, per, scan_b[p].prior, (slot - 1) * lanes_per)

    final = pairs - 1
    loads[0].wait()
    loads[1].wait()
    project_own(0)
    loads[2].wait()
    project_own(1)
    states(0, 0, heads, scan_a.state, 0)
    scan_a.begin()
    go(2, 0, 0)
    loads[3].wait()
    project_own(2)
    go(4, 1, 0)
    part = max(1, heads // 4)
    inner(0, 0, part)
    go(5, 2, 0)
    scan_a.middle()
    for i in range(1, heads // part):
        inner(0, i * part, part)
        go(5 + i, 2 + i, i - 1)
    scan_a.last()
    go(8, 6, 4)
    ready(0, 0)
    project(0, 0)
    if pairs == 1:
        go(8, 8, 8)
    ready(1, 0)
    project(1, 0)
    states_b(0)
    go(9, 7, 6)
    if pairs > 1:
        go(9, 8, 8)
        ready(0, final)
        project(0, final)
        ready(1, final)
        project(1, final)
        states_b(final)
    go(11, 9, 8)
    scan_b[0].middle()
    scan_a.end()
    finish(0, 0, heads, scan_a.prior, 0)
    go(13, 11, 9)
    if pairs > 1:
        scan_b[final].middle()
    loads[4].wait()
    join_own()
    go(15, 13, 11)
    scan_b[0].last()
    go(15, 14, 12)
    ready(2, 0)
    project(2, 0)
    inner_b(0)
    if pairs > 1:
        scan_b[final].last()
    go(15, 15, 13)
    if pairs > 1:
        ready(2, final)
        project(2, final)
        inner_b(final)
    finish_b(0)
    go(16, 16, 16)
    ready(3, 0)
    join(0)
    if pairs > 1:
        finish_b(final)
        ready(3, final)
        join(final)
    for copy in sent:
        copy.wait_send()
    for scan in scans:
        scan.close()


def body(n, seqs, tokens, w_query, w_key, w_value, w_out, norm_gain):
    length, width = tokens.shape[1:]
    cols = w_query.shape[1]
    depth = w_out.shape[0]
    lanes_per = min(256, cols)
    pairs = cols // lanes_per
    parts = 2 if n <= 2 else 1
    outer = seqs // PLANE
    any_spec = pl.BlockSpec(memory_space=pl.ANY)
    vmem = pl.BlockSpec(memory_space=pltpu.VMEM)
    scans = []
    for rows in [cols] + [(n - 1) * lanes_per] * pairs:
        share = rows // PLANE
        scans += [
            pltpu.VMEM((rows, DH), F32),
            pltpu.VMEM((rows, DH), BF16),
            pltpu.VMEM((rows, DH), BF16),
            pltpu.VMEM((PLANE - 1, share, DH), BF16),
            pltpu.VMEM((share, DH), BF16),
            pltpu.VMEM((outer - 1, share, DH), BF16),
            pltpu.VMEM((PLANE - 1, share, DH), BF16),
            pltpu.SemaphoreType.DMA((2 * (PLANE - 1) + outer - 1,)),
            pltpu.SemaphoreType.DMA((2 * (PLANE - 1) + outer - 1,)),
        ]
    out = pl.pallas_call(
        functools.partial(kernel, n, seqs, parts),
        out_shape=jax.ShapeDtypeStruct((length, width), BF16),
        in_specs=[any_spec] * 5 + [vmem],
        out_specs=vmem,
        scratch_shapes=[
            pltpu.VMEM((length, width), BF16),
            pltpu.VMEM((3, width, cols), BF16),
            pltpu.VMEM((depth, width), BF16),
            pltpu.VMEM((n - 1, 3, pairs, width, lanes_per), BF16),
            pltpu.VMEM((n - 1, depth, width), BF16),
            pltpu.VMEM((3, n, length, cols), BF16),
            pltpu.VMEM((n, length, cols), F32),
            pltpu.VMEM((n, length, cols), BF16),
            pltpu.VMEM((length, width), F32),
        ]
        + [pltpu.SemaphoreType.DMA((5,))]
        + [pltpu.SemaphoreType.DMA((8, 4, n - 1, pairs, parts))] * 2
        + scans,
        compiler_params=pltpu.CompilerParams(
            collective_id=0, has_side_effects=True, vmem_limit_bytes=67043328
        ),
    )(tokens[0], w_query, w_key, w_value, w_out, norm_gain.reshape(-1, DH))
    return out[None]


def solution(mesh):
    in_specs = (
        P("dp", "seq", None),
        P(None, "dp"),
        P(None, "dp"),
        P(None, "dp"),
        P("dp", None),
        P(),
    )
    out_specs = P("dp", "seq", None)
    fn = functools.partial(body, mesh.shape["dp"], mesh.shape["seq"])
    return jax.shard_map(fn, mesh=mesh, in_specs=in_specs, out_specs=out_specs, check_vma=False)
```

```python
import functools

import jax
import jax.numpy as jnp
from jax import lax
from jax.experimental import pallas as pl
from jax.experimental.pallas import tpu as pltpu
from jax.sharding import PartitionSpec as P

DH = 128
GROUP = 8
PLANE = 4
LAG = 4
HALVES = {(0, 1): "x", (1, 1): "z"}
MESH = pl.DeviceIdType.MESH
F32 = jnp.float32
BF16 = jnp.bfloat16


class Scan:
    def __init__(self, seq, outer, state, prior, out1, in1, total, in2, out3, sends, recvs):
        self.seq, self.outer = seq, outer
        self.state, self.prior = state, prior
        self.out1, self.in1, self.total, self.in2, self.out3 = out1, in1, total, in2, out3
        self.sends, self.recvs = sends, recvs
        self.share = state.shape[0] // PLANE
        self.me = lax.rem(seq, PLANE)
        self.row = seq // PLANE
        self.mine = self.rows(self.me)
        self.up, self.across, self.down = [], [], []

    def rows(self, owner):
        return pl.ds(pl.multiple_of(owner * self.share, 16), self.share)

    def copy(self, src, dst, index, target):
        return pltpu.make_async_remote_copy(
            src_ref=src,
            dst_ref=dst,
            send_sem=self.sends.at[index],
            recv_sem=self.recvs.at[index],
            device_id={"seq": target},
            device_id_type=MESH,
        )

    def plane(self, k):
        return lax.rem(self.me + k, PLANE)

    def begin(self):
        self.out1[...] = self.state[...].astype(BF16)
        for k in range(1, PLANE):
            target = self.plane(k)
            copy = self.copy(
                self.out1.at[self.rows(target), :], self.in1.at[k - 1], k - 1, self.seq - self.me + target
            )
            copy.start()
            self.up.append(copy)

    def middle(self):
        for copy in self.up:
            copy.wait_recv()
        total = self.state[self.mine, :]
        for k in range(1, PLANE):
            total = total + self.in1[k - 1].astype(F32)
        self.total[...] = total.astype(BF16)
        for k in range(1, self.outer):
            copy = self.copy(self.total, self.in2.at[k - 1], PLANE - 2 + k, self.seq + k * PLANE)
            pl.when(self.row + k < self.outer)(copy.start)
            self.across.append(copy)

    def last(self):
        before = jnp.zeros((self.share, DH), F32)
        for k in range(1, self.outer):
            pl.when(self.row >= k)(self.across[k - 1].wait_recv)
            before = before + jnp.where(self.row >= k, self.in2[k - 1].astype(F32), 0.0)
        parts = [(self.me, self.state[self.mine, :])]
        for k in range(1, PLANE):
            parts.append((self.plane(PLANE - k), self.in1[k - 1].astype(F32)))

        def prefix(target):
            result = before
            for source, part in parts:
                result = result + jnp.where(source < target, part, 0.0)
            return result.astype(BF16)

        for k in range(1, PLANE):
            target = self.plane(k)
            self.out3[k - 1] = prefix(target)
            copy = self.copy(
                self.out3.at[k - 1], self.prior.at[self.mine, :], PLANE - 3 + self.outer + k,
                self.seq - self.me + target,
            )
            copy.start()
            self.down.append(copy)
        self.prior[self.mine, :] = prefix(self.me)

    def end(self):
        for copy in self.down:
            copy.wait_recv()

    def close(self):
        for copy in self.up + self.down:
            copy.wait_send()
        for k in range(1, self.outer):
            pl.when(self.row + k < self.outer)(self.across[k - 1].wait_send)


def kernel(
    n, seqs, parts,
    tok_hbm, wq_hbm, wk_hbm, wv_hbm, wo_hbm, gain_ref, out_ref,
    tok, own, own_o, wide, wide_o, kvq, within, normed, acc,
    load_sem, sends, recvs, *scan_refs,
):
    dp, seq = lax.axis_index("dp"), lax.axis_index("seq")
    length, width = tok.shape
    cols = own.shape[2]
    pairs, lanes_per = wide.shape[2], wide.shape[4]
    outer = seqs // PLANE
    sources = [wk_hbm, wv_hbm, wq_hbm, wo_hbm]
    rank = lax.rem(seq, GROUP)
    core = lax.rem(seq, 2)
    xbit = lax.rem(seq // 2, 2)
    core_mate = seq + 1 - 2 * core
    x_mate = seq + 2 * (1 - 2 * xbit)
    zbit = lax.rem(seq // 4, 2)
    z_mate = seq + 4 * (1 - 2 * zbit)
    x_rank = rank + 2 * (1 - 2 * xbit)
    z_rank = rank + 4 * (1 - 2 * zbit)
    g_rank = z_rank + 2 * (1 - 2 * xbit)
    lanes = ("y", "x", "z", "g", "c0", "c1", "c2", "c3")

    loads = [pltpu.make_async_copy(tok_hbm, tok, load_sem.at[4])]
    for kind in range(4):
        dst = own.at[kind] if kind < 3 else own_o
        loads.append(pltpu.make_async_copy(sources[kind], dst, load_sem.at[kind]))
    for copy in loads:
        copy.start()

    barrier = pltpu.get_barrier_semaphore()
    for slot in range(1, n):
        pl.semaphore_signal(barrier, inc=1, device_id={"dp": lax.rem(dp + slot, n)}, device_id_type=MESH)
    for k in range(1, outer):
        pl.semaphore_signal(barrier, inc=1, device_id={"seq": lax.rem(seq + k * PLANE, seqs)}, device_id_type=MESH)
    place_in = lax.rem(seq, PLANE)
    for k in range(1, PLANE):
        mate = seq - place_in + lax.rem(place_in + k, PLANE)
        pl.semaphore_signal(barrier, inc=1, device_id={"seq": mate}, device_id_type=MESH)
    pl.semaphore_wait(barrier, n - 1 + outer - 1 + PLANE - 1)

    def halves(piece):
        return HALVES.get((piece[0], piece[2]))

    def rank_of(piece):
        axis = halves(piece)
        return {"x": core + 2 * xbit, "z": core + 2 * zbit, None: rank}[axis]

    def mate_of(piece):
        axis = halves(piece)
        return core + 2 * (1 - (xbit if axis == "x" else zbit))

    def rows_of(piece, who):
        kind, _, p, s = piece
        region = (width if kind < 3 else lanes_per) // parts
        size = region // (4 if halves(piece) else GROUP)
        base = s * region + (p * lanes_per if kind == 3 else 0)
        return pl.ds(pl.multiple_of(base + who * size, 16), size)

    def place(piece, rows):
        kind, slot, p, _ = piece
        if kind < 3:
            return wide.at[slot - 1, kind, p, rows, :]
        return wide_o.at[slot - 1, rows, :]

    order, mark = [], {}
    for kinds in ((0, 1), (2,), (3,)):
        for p in range(pairs):
            for kind in kinds:
                order += [(kind, slot, p, s) for s in range(parts) for slot in range(1, n)]
                mark[kind, p] = len(order)
    remote, sent = {}, []

    def push(src, dst, index, target):
        copy = pltpu.make_async_remote_copy(
            src_ref=src, dst_ref=dst, send_sem=sends.at[index], recv_sem=recvs.at[index],
            device_id=target, device_id_type=MESH,
        )
        copy.start()
        sent.append(copy)
        return copy

    def index_of(name, piece):
        kind, slot, p, s = piece
        return (lanes.index(name), kind, slot - 1, p, s)

    for piece in order:
        kind, slot, p, _ = piece
        rows = rows_of(piece, rank_of(piece))
        if kind < 3:
            src = sources[kind].at[rows, pl.ds(p * lanes_per, lanes_per)]
        else:
            src = sources[kind].at[rows, :]
        remote["y", piece] = push(src, place(piece, rows), index_of("y", piece), {"dp": lax.rem(dp - slot + n, n)})

    def forward(name, piece, who, target):
        here = place(piece, rows_of(piece, who))
        remote[name, piece] = push(here, here, index_of(name, piece), {"seq": target})

    def relay(piece):
        remote["y", piece].wait_recv()
        axis, who = halves(piece), rank_of(piece)
        if axis != "z":
            forward("x", piece, who, x_mate)
        if axis != "x":
            forward("z", piece, who, z_mate)
        forward("c0", piece, who, core_mate)

    def relay_again(piece):
        axis = halves(piece)
        if axis:
            remote[axis, piece].wait_recv()
            forward("c1", piece, mate_of(piece), core_mate)
            return
        even = (piece[1] + piece[3]) % 2 == 1
        remote["x", piece].wait_recv()
        if even:
            forward("g", piece, x_rank, z_mate)
        forward("c1", piece, x_rank, core_mate)
        remote["z", piece].wait_recv()
        if not even:
            forward("g", piece, z_rank, x_mate)
        forward("c2", piece, z_rank, core_mate)

    def relay_last(piece):
        if halves(piece):
            return
        remote["g", piece].wait_recv()
        forward("c3", piece, g_rank, core_mate)

    acts = (relay, relay_again, relay_last)
    done = [0, 0, 0]

    def go(*goals):
        goals = [max(at, goal * len(order) // 16) for at, goal in zip(done, goals)]
        goals[0] = max(goals)
        goals[1] = max(goals[1:])
        while any(at < goal for at, goal in zip(done, goals)):
            todo = [i for i in range(3) if done[i] < goals[i] and (i == 0 or done[i] < done[i - 1])]
            pick = min(todo, key=lambda i: done[i] + LAG * i)
            acts[pick](order[done[pick]])
            done[pick] += 1

    def ready(kind, p):
        if done[2] < mark[kind, p]:
            top = -(-mark[kind, p] * 16 // len(order))
            go(top, top, 0 if HALVES.get((kind, p)) else top)
        for piece in order:
            if (piece[0], piece[2]) == (kind, p):
                for name in ("c0", "c1") if halves(piece) else ("c0", "c1", "c2", "c3"):
                    remote[name, piece].wait_recv()

    def lane(i, size):
        return pl.ds(pl.multiple_of(i * size, 128), size)

    def project_own(kind):
        @pl.loop(0, pairs)
        def _(p):
            at = lane(p, lanes_per)
            kvq[kind, 0, :, at] = jnp.dot(tok[...], own[kind, :, at], preferred_element_type=F32).astype(BF16)

    def project(kind, p):
        for slot in range(1, n):
            at = pl.ds(p * lanes_per, lanes_per)
            kvq[kind, slot, :, at] = jnp.dot(
                tok[...], wide[slot - 1, kind, p], preferred_element_type=F32
            ).astype(BF16)

    per = lanes_per // DH

    def states(slot, first, count, ref, base):
        @pl.loop(0, count)
        def _(h):
            at = lane(first + h, DH)
            ref[pl.ds(pl.multiple_of(base + h * DH, DH), DH), :] = lax.dot_general(
                kvq[0, slot, :, at], kvq[1, slot, :, at], (((0,), (0,)), ((), ())), preferred_element_type=F32
            )

    half = length // 2

    def inner(slot, first, count):
        @pl.loop(0, count)
        def _(h):
            at = lane(first + h, DH)
            for begin in (0, half):
                end = begin + half
                scores = lax.dot_general(
                    kvq[2, slot, begin:end, at], kvq[0, slot, :end, at], (((1,), (1,)), ((), ())),
                    preferred_element_type=F32,
                )
                row = begin + lax.broadcasted_iota(jnp.int32, (half, end), 0)
                col = lax.broadcasted_iota(jnp.int32, (half, end), 1)
                scores = jnp.where(col <= row, scores, 0.0).astype(BF16)
                within[slot, begin:end, at] = jnp.dot(
                    scores, kvq[1, slot, :end, at], preferred_element_type=F32
                )

    heads = cols // DH

    def finish(slot, first, count, prior, base):
        owner = lax.rem(dp + slot, n)

        @pl.loop(0, count)
        def _(h):
            at = lane(first + h, DH)
            carried = jnp.dot(
                kvq[2, slot, :, at], prior[pl.ds(pl.multiple_of(base + h * DH, DH), DH), :],
                preferred_element_type=F32,
            )
            mixed = within[slot, :, at] + carried
            scale = lax.rsqrt(jnp.sum(mixed * mixed, axis=-1, keepdims=True) * (1.0 / DH) + 1e-05)
            gain = gain_ref[pl.ds(owner * heads + first + h, 1), :]
            normed[slot, :, at] = (mixed * scale * gain).astype(BF16)

    def join_own():
        @pl.loop(0, width // 256)
        def _(i):
            at = lane(i, 256)
            acc[:, at] = jnp.dot(normed[0], own_o[:, at], preferred_element_type=F32)

    def join(p):
        for slot in range(1, n):
            @pl.loop(0, width // 256)
            def _(i):
                at = lane(i, 256)
                span = pl.ds(p * lanes_per, lanes_per)
                part = acc[:, at] + jnp.dot(
                    normed[slot, :, span], wide_o[slot - 1, span, at], preferred_element_type=F32
                )
                if slot == n - 1 and p == pairs - 1:
                    out_ref[:, at] = part.astype(BF16)
                else:
                    acc[:, at] = part

    size = len(scan_refs) // (1 + pairs)
    scans = [Scan(seq, outer, *scan_refs[i * size:(i + 1) * size]) for i in range(1 + pairs)]
    scan_a, scan_b = scans[0], scans[1:]

    def states_b(p):
        for slot in range(1, n):
            states(slot, p * per, per, scan_b[p].state, (slot - 1) * lanes_per)
        scan_b[p].begin()

    def inner_b(p):
        for slot in range(1, n):
            inner(slot, p * per, per)

    def finish_b(p):
        scan_b[p].end()
        for slot in range(1, n):
            finish(slot, p * per, per, scan_b[p].prior, (slot - 1) * lanes_per)

    final = pairs - 1
    part = max(1, heads // 4)
    pieces = iter(range(heads // part))

    def inner_next():
        for i in pieces:
            inner(0, i * part, part)
            return

    loads[0].wait()
    loads[1].wait()
    project_own(0)
    loads[2].wait()
    project_own(1)
    states(0, 0, heads, scan_a.state, 0)
    scan_a.begin()
    go(2, 0, 0)
    loads[3].wait()
    project_own(2)
    go(4, 0, 0)
    inner_next()
    go(5, 2, 0)
    inner_next()
    scan_a.middle()
    go(6, 4, 0)
    inner_next()
    go(7, 4, 1)
    inner_next()
    go(8, 5, 3)
    go(9, 5, 3)
    ready(0, 0)
    project(0, 0)
    go(10, 6, 3)
    scan_a.last()
    go(12, 7, 4)
    if pairs > 1:
        ready(0, final)
        project(0, final)
    ready(1, 0)
    project(1, 0)
    states_b(0)
    go(14, 9, 4)
    if pairs > 1:
        ready(1, final)
        project(1, final)
        states_b(final)
    go(16, 10, 8)
    scan_a.end()
    finish(0, 0, heads, scan_a.prior, 0)
    go(16, 12, 9)
    scan_b[0].middle()
    loads[4].wait()
    join_own()
    go(16, 13, 10)
    if pairs > 1:
        scan_b[final].middle()
    ready(2, 0)
    project(2, 0)
    inner_b(0)
    go(16, 15, 11)
    scan_b[0].last()
    if pairs > 1:
        ready(2, final)
        project(2, final)
        inner_b(final)
        scan_b[final].last()
    go(16, 16, 14)
    finish_b(0)
    ready(3, 0)
    join(0)
    go(16, 16, 16)
    if pairs > 1:
        finish_b(final)
        ready(3, final)
        join(final)
    for copy in sent:
        copy.wait_send()
    for scan in scans:
        scan.close()


def body(n, seqs, tokens, w_query, w_key, w_value, w_out, norm_gain):
    length, width = tokens.shape[1:]
    cols = w_query.shape[1]
    depth = w_out.shape[0]
    lanes_per = min(256, cols)
    pairs = cols // lanes_per
    parts = 2 if n <= 2 else 1
    outer = seqs // PLANE
    any_spec = pl.BlockSpec(memory_space=pl.ANY)
    vmem = pl.BlockSpec(memory_space=pltpu.VMEM)
    scans = []
    for rows in [cols] + [(n - 1) * lanes_per] * pairs:
        share = rows // PLANE
        scans += [
            pltpu.VMEM((rows, DH), F32),
            pltpu.VMEM((rows, DH), BF16),
            pltpu.VMEM((rows, DH), BF16),
            pltpu.VMEM((PLANE - 1, share, DH), BF16),
            pltpu.VMEM((share, DH), BF16),
            pltpu.VMEM((outer - 1, share, DH), BF16),
            pltpu.VMEM((PLANE - 1, share, DH), BF16),
            pltpu.SemaphoreType.DMA((2 * (PLANE - 1) + outer - 1,)),
            pltpu.SemaphoreType.DMA((2 * (PLANE - 1) + outer - 1,)),
        ]
    out = pl.pallas_call(
        functools.partial(kernel, n, seqs, parts),
        out_shape=jax.ShapeDtypeStruct((length, width), BF16),
        in_specs=[any_spec] * 5 + [vmem],
        out_specs=vmem,
        scratch_shapes=[
            pltpu.VMEM((length, width), BF16),
            pltpu.VMEM((3, width, cols), BF16),
            pltpu.VMEM((depth, width), BF16),
            pltpu.VMEM((n - 1, 3, pairs, width, lanes_per), BF16),
            pltpu.VMEM((n - 1, depth, width), BF16),
            pltpu.VMEM((3, n, length, cols), BF16),
            pltpu.VMEM((n, length, cols), F32),
            pltpu.VMEM((n, length, cols), BF16),
            pltpu.VMEM((length, width), F32),
        ]
        + [pltpu.SemaphoreType.DMA((5,))]
        + [pltpu.SemaphoreType.DMA((8, 4, n - 1, pairs, parts))] * 2
        + scans,
        compiler_params=pltpu.CompilerParams(
            collective_id=0, has_side_effects=True, vmem_limit_bytes=67043328
        ),
    )(tokens[0], w_query, w_key, w_value, w_out, norm_gain.reshape(-1, DH))
    return out[None]


def solution(mesh):
    in_specs = (
        P("dp", "seq", None),
        P(None, "dp"),
        P(None, "dp"),
        P(None, "dp"),
        P("dp", None),
        P(),
    )
    out_specs = P("dp", "seq", None)
    fn = functools.partial(body, mesh.shape["dp"], mesh.shape["seq"])
    return jax.shard_map(fn, mesh=mesh, in_specs=in_specs, out_specs=out_specs, check_vma=False)
```

```python
import functools

import jax
import jax.numpy as jnp
from jax import lax
from jax.experimental import pallas as pl
from jax.experimental.pallas import tpu as pltpu
from jax.sharding import PartitionSpec as P

DH = 128
GROUP = 8
PLANE = 4
LAG = 4
ROUTES = {(0, 1): "x", (1, 1): "z", (3, 0): "y", (3, 1): "y"}
MESH = pl.DeviceIdType.MESH
F32 = jnp.float32
BF16 = jnp.bfloat16


class Scan:
    def __init__(self, seq, outer, state, prior, out1, in1, total, in2, out3, sends, recvs):
        self.seq, self.outer = seq, outer
        self.state, self.prior = state, prior
        self.out1, self.in1, self.total, self.in2, self.out3 = out1, in1, total, in2, out3
        self.sends, self.recvs = sends, recvs
        self.share = state.shape[0] // PLANE
        self.me = lax.rem(seq, PLANE)
        self.row = seq // PLANE
        self.mine = self.rows(self.me)
        self.up, self.across, self.down = [], [], []

    def rows(self, owner):
        return pl.ds(pl.multiple_of(owner * self.share, 16), self.share)

    def copy(self, src, dst, index, target):
        return pltpu.make_async_remote_copy(
            src_ref=src,
            dst_ref=dst,
            send_sem=self.sends.at[index],
            recv_sem=self.recvs.at[index],
            device_id={"seq": target},
            device_id_type=MESH,
        )

    def plane(self, k):
        return lax.rem(self.me + k, PLANE)

    def begin(self):
        self.out1[...] = self.state[...].astype(BF16)
        for k in range(1, PLANE):
            target = self.plane(k)
            copy = self.copy(
                self.out1.at[self.rows(target), :], self.in1.at[k - 1], k - 1, self.seq - self.me + target
            )
            copy.start()
            self.up.append(copy)

    def middle(self):
        for copy in self.up:
            copy.wait_recv()
        total = self.state[self.mine, :]
        for k in range(1, PLANE):
            total = total + self.in1[k - 1].astype(F32)
        self.total[...] = total.astype(BF16)
        for k in range(1, self.outer):
            copy = self.copy(self.total, self.in2.at[k - 1], PLANE - 2 + k, self.seq + k * PLANE)
            pl.when(self.row + k < self.outer)(copy.start)
            self.across.append(copy)

    def last(self):
        before = jnp.zeros((self.share, DH), F32)
        for k in range(1, self.outer):
            pl.when(self.row >= k)(self.across[k - 1].wait_recv)
            before = before + jnp.where(self.row >= k, self.in2[k - 1].astype(F32), 0.0)
        parts = [(self.me, self.state[self.mine, :])]
        for k in range(1, PLANE):
            parts.append((self.plane(PLANE - k), self.in1[k - 1].astype(F32)))

        def prefix(target):
            result = before
            for source, part in parts:
                result = result + jnp.where(source < target, part, 0.0)
            return result.astype(BF16)

        for k in range(1, PLANE):
            target = self.plane(k)
            self.out3[k - 1] = prefix(target)
            copy = self.copy(
                self.out3.at[k - 1], self.prior.at[self.mine, :], PLANE - 3 + self.outer + k,
                self.seq - self.me + target,
            )
            copy.start()
            self.down.append(copy)
        self.prior[self.mine, :] = prefix(self.me)

    def end(self):
        for copy in self.down:
            copy.wait_recv()

    def close(self):
        for copy in self.up + self.down:
            copy.wait_send()
        for k in range(1, self.outer):
            pl.when(self.row + k < self.outer)(self.across[k - 1].wait_send)


def kernel(
    n, seqs, parts,
    tok_hbm, wq_hbm, wk_hbm, wv_hbm, wo_hbm, gain_hbm, out_ref,
    tok, own, own_o, wide, wide_o, kvq, within, normed, acc,
    gain_ref, load_sem, enter, sends, recvs, *scan_refs,
):
    dp, seq = lax.axis_index("dp"), lax.axis_index("seq")
    length, width = tok.shape
    cols = own.shape[2]
    pairs, lanes_per = wide.shape[2], wide.shape[4]
    outer = seqs // PLANE
    sources = [wk_hbm, wv_hbm, wq_hbm, wo_hbm]
    rank = lax.rem(seq, GROUP)
    core = lax.rem(seq, 2)
    xbit = lax.rem(seq // 2, 2)
    core_mate = seq + 1 - 2 * core
    x_mate = seq + 2 * (1 - 2 * xbit)
    zbit = lax.rem(seq // 4, 2)
    z_mate = seq + 4 * (1 - 2 * zbit)
    x_rank = rank + 2 * (1 - 2 * xbit)
    z_rank = rank + 4 * (1 - 2 * zbit)
    g_rank = z_rank + 2 * (1 - 2 * xbit)
    lanes = ("y", "x", "z", "g", "c0", "c1", "c2", "c3")

    loads = [pltpu.make_async_copy(tok_hbm, tok, load_sem.at[4])]
    for kind in range(4):
        dst = own.at[kind] if kind < 3 else own_o
        loads.append(pltpu.make_async_copy(sources[kind], dst, load_sem.at[kind]))
    loads.append(pltpu.make_async_copy(gain_hbm, gain_ref, load_sem.at[5]))
    for copy in loads:
        copy.start()

    barrier = pltpu.get_barrier_semaphore()
    for slot in range(1, n):
        pl.semaphore_signal(barrier, inc=1, device_id={"dp": lax.rem(dp + slot, n)}, device_id_type=MESH)
    row = seq // PLANE
    above, below = row + 1 < outer, row >= 1

    def tell(sem, target):
        pl.semaphore_signal(sem, inc=1, device_id={"seq": target}, device_id_type=MESH)

    pl.when(above)(lambda: tell(barrier, seq + PLANE))
    pl.when(below)(lambda: tell(barrier, seq - PLANE))
    place_in = lax.rem(seq, PLANE)
    for k in range(1, PLANE):
        mate = seq - place_in + lax.rem(place_in + k, PLANE)
        pl.semaphore_signal(barrier, inc=1, device_id={"seq": mate}, device_id_type=MESH)
    pl.semaphore_wait(barrier, n - 1 + PLANE - 1 + above.astype(jnp.int32) + below.astype(jnp.int32))

    def learn(k):
        pl.when(below & (row + k - 1 < outer))(lambda: tell(enter, seq - PLANE))
        pl.when(row + k < outer)(lambda: pl.semaphore_wait(enter, 1))

    def route(piece):
        return ROUTES.get((piece[0], piece[2]))

    def rank_of(piece):
        axis = route(piece)
        return {"x": core + 2 * xbit, "z": core + 2 * zbit, "y": core, None: rank}[axis]

    def mate_of(piece):
        axis = route(piece)
        return core + 2 * (1 - (xbit if axis == "x" else zbit))

    def rows_of(piece, who):
        kind, _, p, s = piece
        region = (width if kind < 3 else lanes_per) // parts
        size = region // {"x": 4, "z": 4, "y": 2, None: GROUP}[route(piece)]
        base = s * region + (p * lanes_per if kind == 3 else 0)
        return pl.ds(pl.multiple_of(base + who * size, 16), size)

    def place(piece, rows):
        kind, slot, p, _ = piece
        if kind < 3:
            return wide.at[slot - 1, kind, p, rows, :]
        return wide_o.at[slot - 1, rows, :]

    order, mark = [], {}
    for kinds in ((0, 1), (2,), (3,)):
        for p in range(pairs):
            for kind in kinds:
                order += [(kind, slot, p, s) for s in range(parts) for slot in range(1, n)]
                mark[kind, p] = len(order)
    remote, sent = {}, []

    def push(src, dst, index, target):
        copy = pltpu.make_async_remote_copy(
            src_ref=src, dst_ref=dst, send_sem=sends.at[index], recv_sem=recvs.at[index],
            device_id=target, device_id_type=MESH,
        )
        copy.start()
        sent.append(copy)
        return copy

    def index_of(name, piece):
        kind, slot, p, s = piece
        return (lanes.index(name), kind, slot - 1, p, s)

    for piece in order:
        kind, slot, p, _ = piece
        rows = rows_of(piece, rank_of(piece))
        if kind < 3:
            src = sources[kind].at[rows, pl.ds(p * lanes_per, lanes_per)]
        else:
            src = sources[kind].at[rows, :]
        remote["y", piece] = push(src, place(piece, rows), index_of("y", piece), {"dp": lax.rem(dp - slot + n, n)})

    def forward(name, piece, who, target):
        here = place(piece, rows_of(piece, who))
        remote[name, piece] = push(here, here, index_of(name, piece), {"seq": target})

    def relay(piece):
        remote["y", piece].wait_recv()
        axis, who = route(piece), rank_of(piece)
        if axis in ("x", None):
            forward("x", piece, who, x_mate)
        if axis in ("z", None):
            forward("z", piece, who, z_mate)
        forward("c0", piece, who, core_mate)

    def relay_again(piece):
        axis = route(piece)
        if axis == "y":
            return
        if axis:
            remote[axis, piece].wait_recv()
            forward("c1", piece, mate_of(piece), core_mate)
            return
        even = (piece[1] + piece[3]) % 2 == 1
        remote["x", piece].wait_recv()
        if even:
            forward("g", piece, x_rank, z_mate)
        forward("c1", piece, x_rank, core_mate)
        remote["z", piece].wait_recv()
        if not even:
            forward("g", piece, z_rank, x_mate)
        forward("c2", piece, z_rank, core_mate)

    def relay_last(piece):
        if route(piece):
            return
        remote["g", piece].wait_recv()
        forward("c3", piece, g_rank, core_mate)

    acts = (relay, relay_again, relay_last)
    done = [0, 0, 0]

    def go(*goals):
        goals = [max(at, goal * len(order) // 16) for at, goal in zip(done, goals)]
        goals[0] = max(goals)
        goals[1] = max(goals[1:])
        while any(at < goal for at, goal in zip(done, goals)):
            todo = [i for i in range(3) if done[i] < goals[i] and (i == 0 or done[i] < done[i - 1])]
            pick = min(todo, key=lambda i: done[i] + LAG * i)
            acts[pick](order[done[pick]])
            done[pick] += 1

    def ready(kind, p):
        if done[2] < mark[kind, p]:
            top = -(-mark[kind, p] * 16 // len(order))
            axis = ROUTES.get((kind, p))
            go(top, 0 if axis == "y" else top, 0 if axis else top)
        for piece in order:
            if (piece[0], piece[2]) == (kind, p):
                for name in ("c0", "c1", "c2", "c3")[:{"y": 1, None: 4}.get(route(piece), 2)]:
                    remote[name, piece].wait_recv()

    def lane(i, size):
        return pl.ds(pl.multiple_of(i * size, 128), size)

    def project_own(kind):
        @pl.loop(0, pairs)
        def _(p):
            at = lane(p, lanes_per)
            kvq[kind, 0, :, at] = jnp.dot(tok[...], own[kind, :, at], preferred_element_type=F32).astype(BF16)

    def project(kind, p):
        for slot in range(1, n):
            at = pl.ds(p * lanes_per, lanes_per)
            kvq[kind, slot, :, at] = jnp.dot(
                tok[...], wide[slot - 1, kind, p], preferred_element_type=F32
            ).astype(BF16)

    per = lanes_per // DH

    def states(slot, first, count, ref, base):
        @pl.loop(0, count)
        def _(h):
            at = lane(first + h, DH)
            ref[pl.ds(pl.multiple_of(base + h * DH, DH), DH), :] = lax.dot_general(
                kvq[0, slot, :, at], kvq[1, slot, :, at], (((0,), (0,)), ((), ())), preferred_element_type=F32
            )

    half = length // 2

    def inner(slot, first, count):
        @pl.loop(0, count)
        def _(h):
            at = lane(first + h, DH)
            for begin in (0, half):
                end = begin + half
                scores = lax.dot_general(
                    kvq[2, slot, begin:end, at], kvq[0, slot, :end, at], (((1,), (1,)), ((), ())),
                    preferred_element_type=F32,
                )
                row = begin + lax.broadcasted_iota(jnp.int32, (half, end), 0)
                col = lax.broadcasted_iota(jnp.int32, (half, end), 1)
                scores = jnp.where(col <= row, scores, 0.0).astype(BF16)
                within[slot, begin:end, at] = jnp.dot(
                    scores, kvq[1, slot, :end, at], preferred_element_type=F32
                )

    heads = cols // DH

    def finish(slot, first, count, prior, base):
        owner = lax.rem(dp + slot, n)

        @pl.loop(0, count)
        def _(h):
            at = lane(first + h, DH)
            carried = jnp.dot(
                kvq[2, slot, :, at], prior[pl.ds(pl.multiple_of(base + h * DH, DH), DH), :],
                preferred_element_type=F32,
            )
            mixed = within[slot, :, at] + carried
            scale = lax.rsqrt(jnp.sum(mixed * mixed, axis=-1, keepdims=True) * (1.0 / DH) + 1e-05)
            gain = gain_ref[pl.ds(owner * heads + first + h, 1), :]
            normed[slot, :, at] = (mixed * scale * gain).astype(BF16)

    def join_own():
        @pl.loop(0, width // 256)
        def _(i):
            at = lane(i, 256)
            acc[:, at] = jnp.dot(normed[0], own_o[:, at], preferred_element_type=F32)

    def join(p):
        for slot in range(1, n):
            @pl.loop(0, width // 256)
            def _(i):
                at = lane(i, 256)
                span = pl.ds(p * lanes_per, lanes_per)
                part = acc[:, at] + jnp.dot(
                    normed[slot, :, span], wide_o[slot - 1, span, at], preferred_element_type=F32
                )
                if slot == n - 1 and p == pairs - 1:
                    out_ref[:, at] = part.astype(BF16)
                else:
                    acc[:, at] = part

    size = len(scan_refs) // (1 + pairs)
    scans = [Scan(seq, outer, *scan_refs[i * size:(i + 1) * size]) for i in range(1 + pairs)]
    scan_a, scan_b = scans[0], scans[1:]

    def states_b(p):
        for slot in range(1, n):
            states(slot, p * per, per, scan_b[p].state, (slot - 1) * lanes_per)
        scan_b[p].begin()

    def inner_b(p):
        for slot in range(1, n):
            inner(slot, p * per, per)

    def finish_b(p):
        scan_b[p].end()
        for slot in range(1, n):
            finish(slot, p * per, per, scan_b[p].prior, (slot - 1) * lanes_per)

    final = pairs - 1
    part = max(1, heads // 4)
    pieces = iter(range(heads // part))

    def inner_next():
        for i in pieces:
            inner(0, i * part, part)
            return

    loads[0].wait()
    loads[1].wait()
    project_own(0)
    loads[2].wait()
    project_own(1)
    states(0, 0, heads, scan_a.state, 0)
    scan_a.begin()
    go(2, 0, 0)
    if outer > 2:
        learn(2)
    loads[3].wait()
    project_own(2)
    go(4, 0, 0)
    inner_next()
    for k in range(3, outer):
        learn(k)
    go(5, 2, 0)
    inner_next()
    scan_a.middle()
    go(6, 4, 0)
    inner_next()
    go(7, 4, 1)
    inner_next()
    go(8, 5, 3)
    go(9, 5, 3)
    ready(0, 0)
    project(0, 0)
    go(10, 6, 3)
    scan_a.last()
    go(12, 7, 4)
    if pairs > 1:
        ready(0, final)
        project(0, final)
    ready(1, 0)
    project(1, 0)
    states_b(0)
    go(12, 9, 4)
    if pairs > 1:
        ready(1, final)
        project(1, final)
        states_b(final)
    go(13, 10, 8)
    scan_a.end()
    loads[5].wait()
    finish(0, 0, heads, scan_a.prior, 0)
    go(13, 12, 9)
    scan_b[0].middle()
    loads[4].wait()
    join_own()
    go(14, 12, 10)
    if pairs > 1:
        scan_b[final].middle()
    ready(2, 0)
    project(2, 0)
    inner_b(0)
    go(14, 12, 11)
    scan_b[0].last()
    if pairs > 1:
        ready(2, final)
        project(2, final)
        inner_b(final)
        scan_b[final].last()
    go(14, 12, 12)
    finish_b(0)
    ready(3, 0)
    join(0)
    go(16, 16, 16)
    if pairs > 1:
        finish_b(final)
        ready(3, final)
        join(final)
    for copy in sent:
        copy.wait_send()
    for scan in scans:
        scan.close()


def body(n, seqs, tokens, w_query, w_key, w_value, w_out, norm_gain):
    length, width = tokens.shape[1:]
    cols = w_query.shape[1]
    depth = w_out.shape[0]
    lanes_per = min(256, cols)
    pairs = cols // lanes_per
    parts = 2 if n <= 2 else 1
    outer = seqs // PLANE
    any_spec = pl.BlockSpec(memory_space=pl.ANY)
    vmem = pl.BlockSpec(memory_space=pltpu.VMEM)
    scans = []
    for rows in [cols] + [(n - 1) * lanes_per] * pairs:
        share = rows // PLANE
        scans += [
            pltpu.VMEM((rows, DH), F32),
            pltpu.VMEM((rows, DH), BF16),
            pltpu.VMEM((rows, DH), BF16),
            pltpu.VMEM((PLANE - 1, share, DH), BF16),
            pltpu.VMEM((share, DH), BF16),
            pltpu.VMEM((outer - 1, share, DH), BF16),
            pltpu.VMEM((PLANE - 1, share, DH), BF16),
            pltpu.SemaphoreType.DMA((2 * (PLANE - 1) + outer - 1,)),
            pltpu.SemaphoreType.DMA((2 * (PLANE - 1) + outer - 1,)),
        ]
    out = pl.pallas_call(
        functools.partial(kernel, n, seqs, parts),
        out_shape=jax.ShapeDtypeStruct((length, width), BF16),
        in_specs=[any_spec] * 6,
        out_specs=vmem,
        scratch_shapes=[
            pltpu.VMEM((length, width), BF16),
            pltpu.VMEM((3, width, cols), BF16),
            pltpu.VMEM((depth, width), BF16),
            pltpu.VMEM((n - 1, 3, pairs, width, lanes_per), BF16),
            pltpu.VMEM((n - 1, depth, width), BF16),
            pltpu.VMEM((3, n, length, cols), BF16),
            pltpu.VMEM((n, length, cols), F32),
            pltpu.VMEM((n, length, cols), BF16),
            pltpu.VMEM((length, width), F32),
        ]
        + [pltpu.VMEM((norm_gain.size // DH, DH), F32), pltpu.SemaphoreType.DMA((6,)), pltpu.SemaphoreType.REGULAR]
        + [pltpu.SemaphoreType.DMA((8, 4, n - 1, pairs, parts))] * 2
        + scans,
        compiler_params=pltpu.CompilerParams(
            collective_id=0, has_side_effects=True, vmem_limit_bytes=67043328
        ),
    )(tokens[0], w_query, w_key, w_value, w_out, norm_gain.reshape(-1, DH))
    return out[None]


def solution(mesh):
    in_specs = (
        P("dp", "seq", None),
        P(None, "dp"),
        P(None, "dp"),
        P(None, "dp"),
        P("dp", None),
        P(),
    )
    out_specs = P("dp", "seq", None)
    fn = functools.partial(body, mesh.shape["dp"], mesh.shape["seq"])
    return jax.shard_map(fn, mesh=mesh, in_specs=in_specs, out_specs=out_specs, check_vma=False)
```

```python
import functools

import jax
import jax.numpy as jnp
from jax import lax
from jax.experimental import pallas as pl
from jax.experimental.pallas import tpu as pltpu
from jax.sharding import PartitionSpec as P

DH = 128
GROUP = 8
PLANE = 4
LAG = 4
ROUTES = {(0, 1, 0): "x", (0, 1, 1): "z", (1, 1, 0): "x", (1, 1, 1): "z", (2, 0, 0): "x", (2, 0, 1): "z", (2, 1, 0): "x", (2, 1, 1): "z", (3, 0, 0): "y", (3, 0, 1): "y", (3, 1, 0): "y", (3, 1, 1): "y"}
MESH = pl.DeviceIdType.MESH
F32 = jnp.float32
BF16 = jnp.bfloat16


class Scan:
    def __init__(self, seq, outer, state, prior, out1, in1, total, in2, out3, sends, recvs):
        self.seq, self.outer = seq, outer
        self.state, self.prior = state, prior
        self.out1, self.in1, self.total, self.in2, self.out3 = out1, in1, total, in2, out3
        self.sends, self.recvs = sends, recvs
        self.share = state.shape[0] // PLANE
        self.me = lax.rem(seq, PLANE)
        self.row = seq // PLANE
        self.mine = self.rows(self.me)
        self.up, self.across, self.down = [], [], []

    def rows(self, owner):
        return pl.ds(pl.multiple_of(owner * self.share, 16), self.share)

    def copy(self, src, dst, index, target):
        return pltpu.make_async_remote_copy(
            src_ref=src,
            dst_ref=dst,
            send_sem=self.sends.at[index],
            recv_sem=self.recvs.at[index],
            device_id={"seq": target},
            device_id_type=MESH,
        )

    def plane(self, k):
        return lax.rem(self.me + k, PLANE)

    def begin(self):
        self.out1[...] = self.state[...].astype(BF16)
        for k in range(1, PLANE):
            target = self.plane(k)
            copy = self.copy(
                self.out1.at[self.rows(target), :], self.in1.at[k - 1], k - 1, self.seq - self.me + target
            )
            copy.start()
            self.up.append(copy)

    def middle(self):
        for copy in self.up:
            copy.wait_recv()
        total = self.state[self.mine, :]
        for k in range(1, PLANE):
            total = total + self.in1[k - 1].astype(F32)
        self.total[...] = total.astype(BF16)
        for k in range(1, self.outer):
            copy = self.copy(self.total, self.in2.at[k - 1], PLANE - 2 + k, self.seq + k * PLANE)
            pl.when(self.row + k < self.outer)(copy.start)
            self.across.append(copy)

    def last(self):
        before = jnp.zeros((self.share, DH), F32)
        for k in range(1, self.outer):
            pl.when(self.row >= k)(self.across[k - 1].wait_recv)
            before = before + jnp.where(self.row >= k, self.in2[k - 1].astype(F32), 0.0)
        parts = [(self.me, self.state[self.mine, :])]
        for k in range(1, PLANE):
            parts.append((self.plane(PLANE - k), self.in1[k - 1].astype(F32)))

        def prefix(target):
            result = before
            for source, part in parts:
                result = result + jnp.where(source < target, part, 0.0)
            return result.astype(BF16)

        for k in range(1, PLANE):
            target = self.plane(k)
            self.out3[k - 1] = prefix(target)
            copy = self.copy(
                self.out3.at[k - 1], self.prior.at[self.mine, :], PLANE - 3 + self.outer + k,
                self.seq - self.me + target,
            )
            copy.start()
            self.down.append(copy)
        self.prior[self.mine, :] = prefix(self.me)

    def end(self):
        for copy in self.down:
            copy.wait_recv()

    def close(self):
        for copy in self.up + self.down:
            copy.wait_send()
        for k in range(1, self.outer):
            pl.when(self.row + k < self.outer)(self.across[k - 1].wait_send)


def kernel(
    n, seqs, parts,
    tok_hbm, wq_hbm, wk_hbm, wv_hbm, wo_hbm, gain_hbm, out_hbm,
    tok, own, own_o, wide, wide_o, kvq, within, normed, acc,
    gain_ref, out_ref, load_sem, enter, sends, recvs, *scan_refs,
):
    dp, seq = lax.axis_index("dp"), lax.axis_index("seq")
    length, width = tok.shape
    cols = own.shape[2]
    pairs, lanes_per = wide.shape[2], wide.shape[4]
    outer = seqs // PLANE
    sources = [wk_hbm, wv_hbm, wq_hbm, wo_hbm]
    rank = lax.rem(seq, GROUP)
    core = lax.rem(seq, 2)
    xbit = lax.rem(seq // 2, 2)
    core_mate = seq + 1 - 2 * core
    x_mate = seq + 2 * (1 - 2 * xbit)
    zbit = lax.rem(seq // 4, 2)
    z_mate = seq + 4 * (1 - 2 * zbit)
    x_rank = rank + 2 * (1 - 2 * xbit)
    z_rank = rank + 4 * (1 - 2 * zbit)
    g_rank = z_rank + 2 * (1 - 2 * xbit)
    lanes = ("y", "x", "z", "g", "c0", "c1", "c2", "c3")

    loads = [pltpu.make_async_copy(tok_hbm, tok, load_sem.at[4])]
    for kind in range(4):
        dst = own.at[kind] if kind < 3 else own_o
        loads.append(pltpu.make_async_copy(sources[kind], dst, load_sem.at[kind]))
    loads.append(pltpu.make_async_copy(gain_hbm, gain_ref, load_sem.at[5]))
    for copy in loads:
        copy.start()

    barrier = pltpu.get_barrier_semaphore()
    for slot in range(1, n):
        pl.semaphore_signal(barrier, inc=1, device_id={"dp": lax.rem(dp + slot, n)}, device_id_type=MESH)
    row = seq // PLANE
    above, below = row + 1 < outer, row >= 1

    def tell(sem, target):
        pl.semaphore_signal(sem, inc=1, device_id={"seq": target}, device_id_type=MESH)

    pl.when(above)(lambda: tell(barrier, seq + PLANE))
    pl.when(below)(lambda: tell(barrier, seq - PLANE))
    place_in = lax.rem(seq, PLANE)
    for k in range(1, PLANE):
        mate = seq - place_in + lax.rem(place_in + k, PLANE)
        pl.semaphore_signal(barrier, inc=1, device_id={"seq": mate}, device_id_type=MESH)
    pl.semaphore_wait(barrier, n - 1 + PLANE - 1 + above.astype(jnp.int32) + below.astype(jnp.int32))

    def learn(k):
        pl.when(below & (row + k - 1 < outer))(lambda: tell(enter, seq - PLANE))
        pl.when(row + k < outer)(lambda: pl.semaphore_wait(enter, 1))

    def route(piece):
        return ROUTES.get((piece[0], piece[2], piece[3]))

    def rank_of(piece):
        axis = route(piece)
        return {"x": core + 2 * xbit, "z": core + 2 * zbit, "y": core, None: rank}[axis]

    def mate_of(piece):
        axis = route(piece)
        return core + 2 * (1 - (xbit if axis == "x" else zbit))

    def rows_of(piece, who):
        kind, _, p, s = piece
        region = (width if kind < 3 else lanes_per) // parts
        size = region // {"x": 4, "z": 4, "y": 2, None: GROUP}[route(piece)]
        base = s * region + (p * lanes_per if kind == 3 else 0)
        return pl.ds(pl.multiple_of(base + who * size, 16), size)

    def place(piece, rows):
        kind, slot, p, _ = piece
        if kind < 3:
            return wide.at[slot - 1, kind, p, rows, :]
        return wide_o.at[slot - 1, rows, :]

    order, mark = [], {}
    for kinds in ((0, 1), (2,), (3,)):
        for p in range(pairs):
            for kind in kinds:
                order += [(kind, slot, p, s) for s in range(parts) for slot in range(1, n)]
                mark[kind, p] = len(order)
    remote, sent = {}, []

    def push(src, dst, index, target):
        copy = pltpu.make_async_remote_copy(
            src_ref=src, dst_ref=dst, send_sem=sends.at[index], recv_sem=recvs.at[index],
            device_id=target, device_id_type=MESH,
        )
        copy.start()
        sent.append(copy)
        return copy

    def index_of(name, piece):
        kind, slot, p, s = piece
        return (lanes.index(name), kind, slot - 1, p, s)

    for piece in order:
        kind, slot, p, _ = piece
        rows = rows_of(piece, rank_of(piece))
        if kind < 3:
            src = sources[kind].at[rows, pl.ds(p * lanes_per, lanes_per)]
        else:
            src = sources[kind].at[rows, :]
        remote["y", piece] = push(src, place(piece, rows), index_of("y", piece), {"dp": lax.rem(dp - slot + n, n)})

    def forward(name, piece, who, target):
        here = place(piece, rows_of(piece, who))
        remote[name, piece] = push(here, here, index_of(name, piece), {"seq": target})

    def relay(piece):
        remote["y", piece].wait_recv()
        axis, who = route(piece), rank_of(piece)
        if axis in ("x", None):
            forward("x", piece, who, x_mate)
        if axis in ("z", None):
            forward("z", piece, who, z_mate)
        forward("c0", piece, who, core_mate)

    def relay_again(piece):
        axis = route(piece)
        if axis == "y":
            return
        if axis:
            remote[axis, piece].wait_recv()
            forward("c1", piece, mate_of(piece), core_mate)
            return
        even = (piece[1] + piece[3]) % 2 == 1
        remote["x", piece].wait_recv()
        if even:
            forward("g", piece, x_rank, z_mate)
        forward("c1", piece, x_rank, core_mate)
        remote["z", piece].wait_recv()
        if not even:
            forward("g", piece, z_rank, x_mate)
        forward("c2", piece, z_rank, core_mate)

    def relay_last(piece):
        if route(piece):
            return
        remote["g", piece].wait_recv()
        forward("c3", piece, g_rank, core_mate)

    acts = (relay, relay_again, relay_last)
    done = [0, 0, 0]

    def go(*goals):
        goals = [max(at, goal * len(order) // 16) for at, goal in zip(done, goals)]
        goals[0] = max(goals)
        goals[1] = max(goals[1:])
        while any(at < goal for at, goal in zip(done, goals)):
            todo = [i for i in range(3) if done[i] < goals[i] and (i == 0 or done[i] < done[i - 1])]
            pick = min(todo, key=lambda i: done[i] + LAG * i)
            acts[pick](order[done[pick]])
            done[pick] += 1

    def ready(kind, p):
        if done[2] < mark[kind, p]:
            top = -(-mark[kind, p] * 16 // len(order))
            used = {route(piece) for piece in order if (piece[0], piece[2]) == (kind, p)}
            go(top, 0 if used == {"y"} else top, top if None in used else 0)
        for piece in order:
            if (piece[0], piece[2]) == (kind, p):
                for name in ("c0", "c1", "c2", "c3")[:{"y": 1, None: 4}.get(route(piece), 2)]:
                    remote[name, piece].wait_recv()

    def lane(i, size):
        return pl.ds(pl.multiple_of(i * size, 128), size)

    def project_own(kind):
        @pl.loop(0, pairs)
        def _(p):
            at = lane(p, lanes_per)
            kvq[kind, 0, :, at] = jnp.dot(tok[...], own[kind, :, at], preferred_element_type=F32).astype(BF16)

    def project(kind, p):
        for slot in range(1, n):
            at = pl.ds(p * lanes_per, lanes_per)
            kvq[kind, slot, :, at] = jnp.dot(
                tok[...], wide[slot - 1, kind, p], preferred_element_type=F32
            ).astype(BF16)

    per = lanes_per // DH

    def states(slot, first, count, ref, base):
        @pl.loop(0, count)
        def _(h):
            at = lane(first + h, DH)
            ref[pl.ds(pl.multiple_of(base + h * DH, DH), DH), :] = lax.dot_general(
                kvq[0, slot, :, at], kvq[1, slot, :, at], (((0,), (0,)), ((), ())), preferred_element_type=F32
            )

    half = length // 2

    def inner(slot, first, count):
        @pl.loop(0, count)
        def _(h):
            at = lane(first + h, DH)
            for begin in (0, half):
                end = begin + half
                scores = lax.dot_general(
                    kvq[2, slot, begin:end, at], kvq[0, slot, :end, at], (((1,), (1,)), ((), ())),
                    preferred_element_type=F32,
                )
                row = begin + lax.broadcasted_iota(jnp.int32, (half, end), 0)
                col = lax.broadcasted_iota(jnp.int32, (half, end), 1)
                scores = jnp.where(col <= row, scores, 0.0).astype(BF16)
                within[slot, begin:end, at] = jnp.dot(
                    scores, kvq[1, slot, :end, at], preferred_element_type=F32
                )

    heads = cols // DH

    def finish(slot, first, count, prior, base):
        owner = lax.rem(dp + slot, n)

        @pl.loop(0, count)
        def _(h):
            at = lane(first + h, DH)
            carried = jnp.dot(
                kvq[2, slot, :, at], prior[pl.ds(pl.multiple_of(base + h * DH, DH), DH), :],
                preferred_element_type=F32,
            )
            mixed = within[slot, :, at] + carried
            scale = lax.rsqrt(jnp.sum(mixed * mixed, axis=-1, keepdims=True) * (1.0 / DH) + 1e-05)
            gain = gain_ref[pl.ds(owner * heads + first + h, 1), :]
            normed[slot, :, at] = (mixed * scale * gain).astype(BF16)

    def join_own():
        @pl.loop(0, width // 256)
        def _(i):
            at = lane(i, 256)
            acc[:, at] = jnp.dot(normed[0], own_o[:, at], preferred_element_type=F32)

    def store(i):
        at = lane(i, 256)
        return pltpu.make_async_copy(out_ref.at[:, at], out_hbm.at[:, at], load_sem.at[6 + i])

    def join(p):
        for slot in range(1, n):
            @pl.loop(0, width // 256)
            def _(i):
                at = lane(i, 256)
                span = pl.ds(p * lanes_per, lanes_per)
                part = acc[:, at] + jnp.dot(
                    normed[slot, :, span], wide_o[slot - 1, span, at], preferred_element_type=F32
                )
                if slot == n - 1 and p == pairs - 1:
                    out_ref[:, at] = part.astype(BF16)
                    store(i).start()
                else:
                    acc[:, at] = part

    size = len(scan_refs) // (1 + pairs)
    scans = [Scan(seq, outer, *scan_refs[i * size:(i + 1) * size]) for i in range(1 + pairs)]
    scan_a, scan_b = scans[0], scans[1:]

    def states_b(p):
        for slot in range(1, n):
            states(slot, p * per, per, scan_b[p].state, (slot - 1) * lanes_per)
        scan_b[p].begin()

    def inner_b(p):
        for slot in range(1, n):
            inner(slot, p * per, per)

    def finish_b(p):
        scan_b[p].end()
        for slot in range(1, n):
            finish(slot, p * per, per, scan_b[p].prior, (slot - 1) * lanes_per)

    final = pairs - 1
    part = max(1, heads // 4)
    pieces = iter(range(heads // part))

    def inner_next():
        for i in pieces:
            inner(0, i * part, part)
            return

    loads[0].wait()
    loads[1].wait()
    project_own(0)
    loads[2].wait()
    project_own(1)
    states(0, 0, heads, scan_a.state, 0)
    scan_a.begin()
    go(2, 0, 0)
    if outer > 2:
        learn(2)
    loads[3].wait()
    project_own(2)
    go(4, 0, 0)
    inner_next()
    for k in range(3, outer):
        learn(k)
    go(5, 2, 0)
    inner_next()
    scan_a.middle()
    go(6, 4, 0)
    inner_next()
    go(7, 4, 1)
    inner_next()
    go(8, 5, 3)
    go(9, 5, 3)
    ready(0, 0)
    project(0, 0)
    go(9, 6, 3)
    scan_a.last()
    go(10, 7, 4)
    if pairs > 1:
        ready(0, final)
        project(0, final)
    ready(1, 0)
    project(1, 0)
    states_b(0)
    go(11, 8, 4)
    if pairs > 1:
        ready(1, final)
        project(1, final)
        states_b(final)
    go(12, 9, 8)
    scan_a.end()
    loads[5].wait()
    finish(0, 0, heads, scan_a.prior, 0)
    go(13, 10, 9)
    scan_b[0].middle()
    loads[4].wait()
    join_own()
    go(13, 11, 10)
    if pairs > 1:
        scan_b[final].middle()
    ready(2, 0)
    project(2, 0)
    inner_b(0)
    go(14, 12, 11)
    scan_b[0].last()
    if pairs > 1:
        ready(2, final)
        project(2, final)
        inner_b(final)
        scan_b[final].last()
    go(14, 12, 12)
    finish_b(0)
    ready(3, 0)
    join(0)
    go(16, 16, 16)
    if pairs > 1:
        finish_b(final)
        ready(3, final)
        join(final)
    for copy in sent:
        copy.wait_send()
    for i in range(width // 256):
        store(i).wait()
    for scan in scans:
        scan.close()


def body(n, seqs, tokens, w_query, w_key, w_value, w_out, norm_gain):
    length, width = tokens.shape[1:]
    cols = w_query.shape[1]
    depth = w_out.shape[0]
    lanes_per = min(256, cols)
    pairs = cols // lanes_per
    parts = 2 if n <= 2 else 1
    outer = seqs // PLANE
    any_spec = pl.BlockSpec(memory_space=pl.ANY)
    scans = []
    for rows in [cols] + [(n - 1) * lanes_per] * pairs:
        share = rows // PLANE
        scans += [
            pltpu.VMEM((rows, DH), F32),
            pltpu.VMEM((rows, DH), BF16),
            pltpu.VMEM((rows, DH), BF16),
            pltpu.VMEM((PLANE - 1, share, DH), BF16),
            pltpu.VMEM((share, DH), BF16),
            pltpu.VMEM((outer - 1, share, DH), BF16),
            pltpu.VMEM((PLANE - 1, share, DH), BF16),
            pltpu.SemaphoreType.DMA((2 * (PLANE - 1) + outer - 1,)),
            pltpu.SemaphoreType.DMA((2 * (PLANE - 1) + outer - 1,)),
        ]
    out = pl.pallas_call(
        functools.partial(kernel, n, seqs, parts),
        out_shape=jax.ShapeDtypeStruct((length, width), BF16),
        in_specs=[any_spec] * 6,
        out_specs=any_spec,
        scratch_shapes=[
            pltpu.VMEM((length, width), BF16),
            pltpu.VMEM((3, width, cols), BF16),
            pltpu.VMEM((depth, width), BF16),
            pltpu.VMEM((n - 1, 3, pairs, width, lanes_per), BF16),
            pltpu.VMEM((n - 1, depth, width), BF16),
            pltpu.VMEM((3, n, length, cols), BF16),
            pltpu.VMEM((n, length, cols), F32),
            pltpu.VMEM((n, length, cols), BF16),
            pltpu.VMEM((length, width), F32),
        ]
        + [pltpu.VMEM((norm_gain.size // DH, DH), F32), pltpu.VMEM((length, width), BF16), pltpu.SemaphoreType.DMA((6 + width // 256,)), pltpu.SemaphoreType.REGULAR]
        + [pltpu.SemaphoreType.DMA((8, 4, n - 1, pairs, parts))] * 2
        + scans,
        compiler_params=pltpu.CompilerParams(
            collective_id=0, has_side_effects=True, vmem_limit_bytes=67043328
        ),
    )(tokens[0], w_query, w_key, w_value, w_out, norm_gain.reshape(-1, DH))
    return out[None]


def solution(mesh):
    in_specs = (
        P("dp", "seq", None),
        P(None, "dp"),
        P(None, "dp"),
        P(None, "dp"),
        P("dp", None),
        P(),
    )
    out_specs = P("dp", "seq", None)
    fn = functools.partial(body, mesh.shape["dp"], mesh.shape["seq"])
    return jax.shard_map(fn, mesh=mesh, in_specs=in_specs, out_specs=out_specs, check_vma=False)
```
